32 devices in a mesh: dp: 2 (over x), row: 4 (over z), col: 4 (over y, core).
Axes of the slice: x: 2, y: 2, z: 4, core: 2. Of those that a mesh axis runs over, the one named last changes fastest.
Arguments:
- block_input: bfloat16 [1024, 1024], P(('dp', 'col'), 'row'), may hold values from -6 to 6
- attn_gain: float32 [1024], P('row'), may hold values from 0.5 to 1.5
- query_weight: bfloat16 [1024, 1024], P('row', 'col'), may hold values from -0.1875 to 0.1875
- key_weight: bfloat16 [1024, 1024], P('row', 'col'), may hold values from -0.1875 to 0.1875
- value_weight: bfloat16 [1024, 2048], P('row', 'col'), may hold values from -0.1875 to 0.1875
- gate_weight: bfloat16 [1024, 2048], P('row', 'col'), may hold values from -0.1875 to 0.1875
- decay_weight: bfloat16 [1024, 8], P('row', 'col'), may hold values from -0.1875 to 0.1875
- beta_weight: bfloat16 [1024, 8], P('row', 'col'), may hold values from -0.1875 to 0.1875
- query_conv: float32 [4, 1024], P(None, 'col'), may hold values from -3 to 3
- key_conv: float32 [4, 1024], P(None, 'col'), may hold values from -3 to 3
- value_conv: float32 [4, 2048], P(None, 'col'), may hold values from -3 to 3
- decay_log: float32 [8], P('col'), may hold values from -4 to 0.5
- decay_bias: float32 [8], P('col'), may hold values from -3 to 0
- head_gain: float32 [256], replicated, may hold values from 0.5 to 1.5
- out_weight: bfloat16 [2048, 1024], P('col', 'row'), may hold values from -0.1875 to 0.1875
- ffn_gain: float32 [1024], P('row'), may hold values from 0.5 to 1.5
- ffn_gate: bfloat16 [1024, 2816], P('row', 'col'), may hold values from -0.1875 to 0.1875
- ffn_up: bfloat16 [1024, 2816], P('row', 'col'), may hold values from -0.1875 to 0.1875
- ffn_down: bfloat16 [2816, 1024], P('col', 'row'), may hold values from -0.15625 to 0.15625
- out_grad: bfloat16 [1024, 1024], P(('dp', 'col'), 'row'), may hold values from -6 to 6
- seq_starts: int32 [8, 1], replicated, may hold values from 0 to 64, as said below
- seq_lengths: int32 [8, 1], replicated, may hold values from 1 to 128, as said below
Outputs:
- output: bfloat16 [1024, 1024], P(('dp', 'col'), 'row')
- input_grad: float32 [1024, 1024], P(('dp', 'col'), 'row')
- attn_gain_grad: float32 [1024], P('row')
- query_weight_grad: float32 [1024, 1024], P('row', 'col')
- key_weight_grad: float32 [1024, 1024], P('row', 'col')
- value_weight_grad: float32 [1024, 2048], P('row', 'col')
- gate_weight_grad: float32 [1024, 2048], P('row', 'col')
- decay_weight_grad: float32 [1024, 8], P('row', 'col')
- beta_weight_grad: float32 [1024, 8], P('row', 'col')
- query_conv_grad: float32 [4, 1024], P(None, 'col')
- key_conv_grad: float32 [4, 1024], P(None, 'col')
- value_conv_grad: float32 [4, 2048], P(None, 'col')
- decay_log_grad: float32 [8], P('col')
- decay_bias_grad: float32 [8], P('col')
- head_gain_grad: float32 [256], replicated
- out_weight_grad: float32 [2048, 1024], P('col', 'row')
- ffn_gain_grad: float32 [1024], P('row')
- ffn_gate_grad: float32 [1024, 2816], P('row', 'col')
- ffn_up_grad: float32 [1024, 2816], P('row', 'col')
- ffn_down_grad: float32 [2816, 1024], P('col', 'row')
The draws below stay inside these ranges and needn't reach their ends.
Inputs may be any that keep to these rules, and one draw needn't show every extreme that they name: `seq_starts`: sequences of a slot are in order and do not intersect; sequence i starts within tokens i * 128 to i * 128 + 128 // 2 of its slot and ends by (i + 1) * 128 - 1; in every draw some sequence starts at the last of these in the slot's last region. `seq_lengths`: in every draw some sequence is 128 tokens long.
All inputs are finite; a program needn't handle non-finite values.
Results may differ from the reference program's by a relative error of at most 0.012.
Values may be sent and summed in bfloat16 or wider, within the bound.
A program may use at most 128 MiB of HBM per device.

```python
import jax
import jax.numpy as jnp
from jax import lax

D = 1024
HEADS = 8
DV = 256
FF = 2816
KCONV = 4
BLOCK = 64
NSEQ = 1
SLOT = 128
SLOTS = 8
TOKENS = 1024
KEYS = 1024
VALS = 2048


def sequence_layout(key):
    region = SLOT // NSEQ
    base = jax.random.fold_in(key, 7)
    key_cap = jax.random.fold_in(base, 1)
    key_len = jax.random.fold_in(base, 2)
    key_off = jax.random.fold_in(base, 3)
    key_pick = jax.random.fold_in(base, 4)
    key_late = jax.random.fold_in(base, 5)
    divisor = 1 + jax.random.randint(key_cap, (SLOTS, 1), 0, 2)
    capacity = region // divisor
    raw_len = jax.random.randint(key_len, (SLOTS, NSEQ), 0, 1 << 20)
    lengths = raw_len % (capacity - capacity // 2 + 1) + capacity // 2
    lengths = jnp.maximum(lengths, 1)
    picked = jax.random.randint(key_pick, (), 0, SLOTS * NSEQ)
    flat_index = jnp.arange(SLOTS * NSEQ, dtype=jnp.int32).reshape(SLOTS, NSEQ)
    late_slot = jax.random.randint(key_late, (), 0, SLOTS)
    late_flat = late_slot * NSEQ + NSEQ - 1
    late_slot = jnp.where(late_flat == picked, (late_slot + 1) % SLOTS, late_slot)
    late_flat = late_slot * NSEQ + NSEQ - 1
    lengths = jnp.where(flat_index == picked, region, lengths)
    lengths = jnp.where(flat_index == late_flat, region // 2, lengths).astype(jnp.int32)
    raw_off = jax.random.randint(key_off, (SLOTS, NSEQ), 0, 1 << 20)
    room = jnp.minimum(region - lengths, region // 2)
    offsets = raw_off % (room + 1)
    offsets = jnp.where(flat_index == late_flat, region // 2, offsets)
    starts = offsets + jnp.arange(NSEQ, dtype=jnp.int32)[None, :] * region
    return (starts.astype(jnp.int32), lengths)


def draw_seq_starts(key, part):
    return sequence_layout(key)[0]


def draw_seq_lengths(key, part):
    return sequence_layout(key)[1]


def shard_levels(stream_key, shape, cuts, smallest, largest):
    level, own = 1.0, jax.random.fold_in(stream_key, 6)
    for dim, blocks in cuts:
        heights = jnp.exp(jax.random.uniform(jax.random.fold_in(own, dim), (blocks,), jnp.float32, smallest / len(cuts), largest / len(cuts)))
        level = level * jnp.repeat(heights, shape[dim] // blocks).reshape([-1 if axis == dim else 1 for axis in range(len(shape))])
    return level


def centred(rng, dims, deviation, reach, split=(), kind=jnp.bfloat16):
    entries = jax.random.normal(rng, dims, jnp.float32) * deviation
    if len(split) > 0:
        entries = shard_levels(rng, dims, split, -0.22, 0.18) * entries
    return jnp.clip(entries, min=-reach, max=reach).astype(kind)


def setup_inputs(seed: int = 0) -> dict:
    arg_keys = jax.random.split(jax.random.key(seed), 23)
    block_input = centred(arg_keys[0], (TOKENS, D), 1.0, 6.0, ((0, 8), (1, 4)))
    attn_gain = jnp.clip(1.0 + 0.1 * jax.random.normal(arg_keys[1], (D,), jnp.float32), 0.5, 1.5)
    query_weight = centred(arg_keys[2], (D, KEYS), D ** -0.5, 0.1875, ((0, 4), (1, 4)))
    key_weight = centred(arg_keys[3], (D, KEYS), D ** -0.5, 0.1875, ((0, 4), (1, 4)))
    value_weight = centred(arg_keys[4], (D, VALS), D ** -0.5, 0.1875, ((0, 4), (1, 4)))
    gate_weight = centred(arg_keys[5], (D, VALS), D ** -0.5, 0.1875, ((0, 4), (1, 4)))
    decay_weight = centred(arg_keys[6], (D, HEADS), D ** -0.5, 0.1875, ((0, 4), (1, 4)))
    beta_weight = centred(arg_keys[7], (D, HEADS), D ** -0.5, 0.1875, ((0, 4), (1, 4)))
    query_conv = centred(arg_keys[8], (KCONV, KEYS), 0.5, 3.0, ((1, 4),), jnp.float32)
    key_conv = centred(arg_keys[9], (KCONV, KEYS), 0.5, 3.0, ((1, 4),), jnp.float32)
    value_conv = centred(arg_keys[10], (KCONV, VALS), 0.5, 3.0, ((1, 4),), jnp.float32)
    decay_log = jnp.clip(-4.0 + 4.5 * jax.random.uniform(arg_keys[11], (HEADS,), jnp.float32) ** shard_levels(arg_keys[11], (HEADS,), ((0, 4),), -0.2, 0.2), -4.0, 0.5)
    decay_bias = jnp.clip(-3.0 + 3.0 * jax.random.uniform(arg_keys[12], (HEADS,), jnp.float32) ** shard_levels(arg_keys[12], (HEADS,), ((0, 4),), -0.2, 0.2), -3.0, 0.0)
    head_gain = jnp.clip(1.0 + 0.1 * jax.random.normal(arg_keys[13], (DV,), jnp.float32), 0.5, 1.5)
    out_weight = centred(arg_keys[14], (VALS, D), D ** -0.5, 0.1875, ((0, 4), (1, 4)))
    ffn_gain = jnp.clip(1.0 + 0.1 * jax.random.normal(arg_keys[15], (D,), jnp.float32), 0.5, 1.5)
    ffn_gate = centred(arg_keys[16], (D, FF), D ** -0.5, 0.1875, ((0, 4), (1, 4)))
    ffn_up = centred(arg_keys[17], (D, FF), D ** -0.5, 0.1875, ((0, 4), (1, 4)))
    ffn_down = centred(arg_keys[18], (FF, D), (FF // 2) ** -0.5, 0.15625, ((0, 4), (1, 4)))
    out_grad = centred(arg_keys[19], (TOKENS, D), 1.0, 6.0, ((0, 8), (1, 4)))
    seq_starts = draw_seq_starts(jax.random.fold_in(arg_keys[22], 71), 0)
    seq_lengths = draw_seq_lengths(jax.random.fold_in(arg_keys[22], 71), 0)
    return dict(block_input=block_input, attn_gain=attn_gain, query_weight=query_weight, key_weight=key_weight, value_weight=value_weight, gate_weight=gate_weight, decay_weight=decay_weight, beta_weight=beta_weight, query_conv=query_conv, key_conv=key_conv, value_conv=value_conv, decay_log=decay_log, decay_bias=decay_bias, head_gain=head_gain, out_weight=out_weight, ffn_gain=ffn_gain, ffn_gate=ffn_gate, ffn_up=ffn_up, ffn_down=ffn_down, out_grad=out_grad, seq_starts=seq_starts, seq_lengths=seq_lengths)


epsilon = 1e-06
highest = lax.Precision.HIGHEST

def segment_info(starts, lengths, count):
    position = jnp.arange(count, dtype=jnp.int32)[:, None]
    begun = (position >= starts[None, :]).astype(jnp.int32)
    ended = (position >= (starts + lengths)[None, :]).astype(jnp.int32)
    segment = lax.optimization_barrier(jnp.sum(begun + ended, axis=1)).astype(jnp.int32)
    inside = lax.optimization_barrier(jnp.sum(begun - ended, axis=1)).astype(jnp.float32)
    return (segment, inside)

def short_conv(signal, kernel, segment):
    length = signal.shape[0]
    tap_count = kernel.shape[0]
    running_total = kernel[tap_count - 1] * signal
    for offset in range(1, tap_count):
        moved = jnp.pad(signal, ((offset, 0), (0, 0)))[:length]
        earlier = jnp.pad(segment, (offset, 0), constant_values=-1)[:length]
        running_total = running_total + kernel[tap_count - 1 - offset] * jnp.where((earlier == segment)[:, None], moved, 0.0)
    return jax.nn.silu(running_total)

def unit_heads(signal, head_count):
    shaped = signal.reshape(signal.shape[0], head_count, -1)
    return shaped * lax.rsqrt(lax.optimization_barrier(jnp.sum(shaped * shaped, axis=-1, keepdims=True)) + epsilon)

def delta_rule(queries, key_heads, value_heads, write_rate, log_decay, segment):
    length, head_count, key_size = queries.shape
    value_size = value_heads.shape[2]
    blocks = length // BLOCK
    position = jnp.arange(BLOCK, dtype=jnp.int32)
    later_mask = position[:, None] > position[None, :]
    upto_mask = position[:, None] >= position[None, :]

    def advance(carry, pieces):
        memory, last_segment = carry
        block_query, block_key, block_value, block_rate, block_decay, block_segment = pieces
        cumulative = jnp.cumsum(block_decay, axis=0)
        same_segment = block_segment[:, None] == block_segment[None, :]
        strict = (same_segment & later_mask).astype(jnp.float32)
        within = (same_segment & upto_mask).astype(jnp.float32)
        carried = (block_segment == last_segment).astype(jnp.float32)
        decay_ratio = jnp.exp(jnp.minimum(cumulative.T[:, :, None] - cumulative.T[:, None, :], 0.0))
        key_dots = jnp.einsum('thd,jhd->htj', block_key, block_key, precision=highest)
        query_dots = jnp.einsum('thd,jhd->htj', block_query, block_key, precision=highest)
        lower_part = block_rate.T[:, :, None] * decay_ratio * key_dots * strict
        decayed = (jnp.exp(cumulative) * carried[:, None]).T
        recalled = jnp.einsum('hvk,thk->htv', memory, block_key, precision=highest)
        target = block_rate.T[:, :, None] * (jnp.transpose(block_value, (1, 0, 2)) - decayed[:, :, None] * recalled)
        writes = jax.scipy.linalg.solve_triangular(lower_part, target, lower=True, unit_diagonal=True)
        readout = decayed[:, :, None] * jnp.einsum('hvk,thk->htv', memory, block_query, precision=highest)
        readout = readout + jnp.einsum('htj,hjv->htv', decay_ratio * query_dots * within, writes, precision=highest)
        closing = (block_segment == block_segment[-1]).astype(jnp.float32)
        ending = jnp.exp(cumulative[-1][None, :] - cumulative) * closing[:, None]
        memory = memory * decayed[:, -1][:, None, None] + jnp.einsum('jh,hjv,jhk->hvk', ending, writes, block_key, precision=highest)
        return ((memory, block_segment[-1]), jnp.transpose(readout, (1, 0, 2)))

    def blocked(array):
        return array.reshape((blocks, BLOCK) + array.shape[1:])
    initial = (jnp.zeros((head_count, value_size, key_size), jnp.float32), jnp.array(-1, jnp.int32))
    final_carry, stacked = lax.scan(advance, initial, (blocked(queries), blocked(key_heads), blocked(value_heads), blocked(write_rate), blocked(log_decay), blocked(segment)))
    return stacked.reshape(length, head_count, value_size)

def token_mixer(linears, params, segment, inside):
    query_lin, key_lin, value_lin, gate_lin, decay_lin, rate_lin = linears
    conv_query, conv_key, conv_value, log_rate, rate_bias, norm_gain = params
    head_count = log_rate.shape[0]
    length = query_lin.shape[0]
    queries = unit_heads(short_conv(query_lin, conv_query, segment), head_count)
    queries = queries * queries.shape[-1] ** (-0.5)
    key_heads = unit_heads(short_conv(key_lin, conv_key, segment), head_count)
    value_heads = short_conv(value_lin, conv_value, segment).reshape(length, head_count, -1)
    write_rate = jax.nn.sigmoid(rate_lin)
    log_decay = -jnp.exp(log_rate) * jax.nn.softplus(decay_lin + rate_bias)
    mixed_heads = delta_rule(queries, key_heads, value_heads, write_rate, log_decay, segment)
    normed = mixed_heads * lax.rsqrt(lax.optimization_barrier(jnp.mean(mixed_heads * mixed_heads, axis=-1, keepdims=True)) + epsilon) * norm_gain
    gate_heads = jax.nn.silu(gate_lin.reshape(length, head_count, -1))
    return (normed * gate_heads * inside[:, None, None]).reshape(length, -1)

def rms_scale(values):
    return lax.rsqrt(lax.optimization_barrier(jnp.mean(values * values, axis=1)) + epsilon)

def rms_backward(values, row_scale, gain_vector, upstream):
    weighted = upstream * gain_vector
    inner_mean = lax.optimization_barrier(jnp.mean(weighted * values, axis=1))
    grad_values = row_scale[:, None] * weighted - values * (row_scale * row_scale * row_scale * inner_mean)[:, None]
    return (grad_values, lax.optimization_barrier(jnp.sum(upstream * values * row_scale[:, None], axis=0)))

def matmul(left, right):
    return jnp.dot(left.astype(jnp.float32), right.astype(jnp.float32), preferred_element_type=jnp.float32)

def left_matmul_result(left, right):
    return jnp.dot(left.T.astype(jnp.float32), right.astype(jnp.float32), preferred_element_type=jnp.float32)

def right_product(left, right):
    return jnp.dot(left.astype(jnp.float32), right.T.astype(jnp.float32), preferred_element_type=jnp.float32)

def reference(block_input, attn_gain, query_weight, key_weight, value_weight, gate_weight, decay_weight, beta_weight, query_conv, key_conv, value_conv, decay_log, decay_bias, head_gain, out_weight, ffn_gain, ffn_gate, ffn_up, ffn_down, out_grad, seq_starts, seq_lengths):
    slot_count = seq_starts.shape[0]
    slot_rows = block_input.shape[0] // slot_count
    feature_count = block_input.shape[1]
    in_weights = (query_weight, key_weight, value_weight, gate_weight, decay_weight, beta_weight)
    mixer_params = (query_conv, key_conv, value_conv, decay_log, decay_bias, head_gain)
    templates = (attn_gain,) + in_weights + mixer_params + (out_weight, ffn_gain, ffn_gate, ffn_up, ffn_down)
    initial = tuple((jnp.zeros(template.shape, jnp.float32) for template in templates))

    def one_slot(grand_totals, slot_data):
        rows_in, row_gradients, starts, lengths = slot_data
        segment, inside = segment_info(starts, lengths, slot_rows)
        inputs = rows_in.astype(jnp.float32)
        first_scale = rms_scale(inputs)
        first_normalized = (inputs * first_scale[:, None] * attn_gain).astype(jnp.bfloat16)
        linears = tuple((matmul(first_normalized, weight) for weight in in_weights))

        def mixer_piece(linear_set, param_set):
            return token_mixer(linear_set, param_set, segment, inside)
        gated, mixer_back = jax.vjp(mixer_piece, linears, mixer_params)
        mixer_output = gated.astype(jnp.bfloat16)
        resid = inputs + matmul(mixer_output, out_weight)
        second_scale = rms_scale(resid)
        second_normalized = (resid * second_scale[:, None] * ffn_gain).astype(jnp.bfloat16)
        gate_part = matmul(second_normalized, ffn_gate)
        up_part = matmul(second_normalized, ffn_up)
        hidden_activation = (jax.nn.silu(gate_part) * up_part * inside[:, None]).astype(jnp.bfloat16)
        output = (resid + matmul(hidden_activation, ffn_down)).astype(jnp.bfloat16)
        grad_hidden = right_product(row_gradients, ffn_down) * inside[:, None]
        sigmoid_gate = jax.nn.sigmoid(gate_part)
        gate_gradient = (grad_hidden * up_part * sigmoid_gate * (1.0 + gate_part * (1.0 - sigmoid_gate))).astype(jnp.bfloat16)
        up_gradient = (grad_hidden * gate_part * sigmoid_gate).astype(jnp.bfloat16)
        grad_second = right_product(gate_gradient, ffn_gate) + right_product(up_gradient, ffn_up)
        resid_part, feedforward_gain_share = rms_backward(resid, second_scale, ffn_gain, grad_second)
        grad_resid = row_gradients.astype(jnp.float32) + resid_part
        residual_signal_path = grad_resid.astype(jnp.bfloat16)
        grad_mixed = right_product(residual_signal_path, out_weight)
        grad_linears, parameter_gradients = mixer_back(grad_mixed)
        linear_signal_path = tuple((gradient.astype(jnp.bfloat16) for gradient in grad_linears))
        grad_first = right_product(linear_signal_path[0], in_weights[0])
        for signal_path_gradient, weight in zip(linear_signal_path[1:], in_weights[1:]):
            grad_first = grad_first + right_product(signal_path_gradient, weight)
        input_part, attention_gain_share = rms_backward(inputs, first_scale, attn_gain, grad_first)
        input_grad = grad_resid + input_part
        summand_terms = (attention_gain_share,) + tuple((left_matmul_result(first_normalized, signal_path_gradient) for signal_path_gradient in linear_signal_path)) + tuple(parameter_gradients) + (left_matmul_result(mixer_output, residual_signal_path), feedforward_gain_share, left_matmul_result(second_normalized, gate_gradient), left_matmul_result(second_normalized, up_gradient), left_matmul_result(hidden_activation, row_gradients))
        grand_totals = tuple((running_total + summand_term for running_total, summand_term in zip(grand_totals, summand_terms)))
        return (grand_totals, (output, input_grad))
    slot_inputs = block_input.reshape(slot_count, slot_rows, feature_count)
    slot_grads = out_grad.reshape(slot_count, slot_rows, feature_count)
    grand_totals, stacked = lax.scan(one_slot, initial, (slot_inputs, slot_grads, seq_starts, seq_lengths))
    output = stacked[0].reshape(-1, feature_count)
    input_grad = stacked[1].reshape(-1, feature_count)
    return (output, input_grad, grand_totals[0], grand_totals[1], grand_totals[2], grand_totals[3], grand_totals[4], grand_totals[5], grand_totals[6], grand_totals[7], grand_totals[8], grand_totals[9], grand_totals[10], grand_totals[11], grand_totals[12], grand_totals[13], grand_totals[14], grand_totals[15], grand_totals[16], grand_totals[17])
```

```python
import jax
import jax.numpy as jnp
from jax import lax
from jax.experimental import pallas as pl
from jax.experimental.pallas import tpu as pltpu
from jax.sharding import PartitionSpec as P

epsilon = 1e-06
highest = lax.Precision.HIGHEST


def fp_dot(left, right, left_dim, right_dim):
    return lax.dot_general(
        left,
        right,
        (((left_dim,), (right_dim,)), ((), ())),
        precision=highest,
        preferred_element_type=jnp.float32,
    )


def plain_softplus(values):
    return jnp.maximum(values, 0.0) + jnp.log1p(jnp.exp(-jnp.abs(values)))


@jax.custom_vjp
def smooth_ramp(values):
    return plain_softplus(values)


smooth_ramp.defvjp(
    lambda values: (plain_softplus(values), values),
    lambda values, upstream: (upstream * lax.logistic(values),),
)


@jax.custom_vjp
def apply_inverse(inverse, lower_part, target):
    return fp_dot(inverse, target, 1, 0)


def apply_inverse_forward(inverse, lower_part, target):
    writes = fp_dot(inverse, target, 1, 0)
    return writes, (inverse, writes)


def apply_inverse_backward(saved, upstream):
    inverse, writes = saved
    grad_target = fp_dot(inverse, upstream, 0, 0)
    return (jnp.zeros_like(inverse), -fp_dot(grad_target, writes, 1, 1), grad_target)


apply_inverse.defvjp(apply_inverse_forward, apply_inverse_backward)


def unit_lower_inverse(lower_part, row_index, column_index):
    length = lower_part.shape[0]
    inverse = jnp.where(row_index == column_index, 1.0, 0.0)
    level = 0
    while (1 << level) < length:
        row_block = row_index >> level
        column_block = column_index >> level
        joined = (row_block == column_block + 1) & ((column_block & 1) == 0)
        corner = jnp.where(joined, lower_part, 0.0)
        if level == 0:
            inverse = inverse - corner
        else:
            inverse = inverse - fp_dot(fp_dot(inverse, corner, 1, 0), inverse, 1, 0)
        level += 1
    return inverse


def slot_masks(bounds_ref, length, tap_count):
    row_index = lax.broadcasted_iota(jnp.int32, (length, length), 0)
    column_index = lax.broadcasted_iota(jnp.int32, (length, length), 1)
    token = lax.broadcasted_iota(jnp.int32, (length, 1), 0)
    row_segment = jnp.zeros((length, length), jnp.int32)
    column_segment = jnp.zeros((length, length), jnp.int32)
    inside = jnp.zeros((length, 1), jnp.float32)
    for i in range(bounds_ref.shape[1]):
        begin = bounds_ref[0, i]
        end = begin + bounds_ref[1, i]
        row_segment += jnp.where(row_index >= begin, 1, 0) + jnp.where(row_index >= end, 1, 0)
        column_segment += jnp.where(column_index >= begin, 1, 0)
        column_segment += jnp.where(column_index >= end, 1, 0)
        inside += jnp.where((token >= begin) & (token < end), 1.0, 0.0)
    same = row_segment == column_segment
    shifts = [
        jnp.where(same & (column_index == row_index - offset), 1.0, 0.0)
        for offset in range(1, tap_count)
    ]
    return dict(
        row_index=row_index,
        column_index=column_index,
        shifts=shifts,
        strict=jnp.where(same & (row_index > column_index), 1.0, 0.0),
        within=jnp.where(same & (row_index >= column_index), 1.0, 0.0),
        upto=jnp.where(row_index >= column_index, 1.0, 0.0),
        later=jnp.where(row_index > column_index, 1.0, 0.0),
        inside=inside,
    )


def conv_head(signal, taps, shifts):
    total = taps[-1] * signal
    for offset, shift in enumerate(shifts, 1):
        total = total + taps[len(taps) - 1 - offset] * fp_dot(shift, signal, 1, 0)
    return total * lax.logistic(total)


def unit_rows(values):
    return values * lax.rsqrt(jnp.sum(values * values, axis=1, keepdims=True) + epsilon)


def mixer_head(masks, inverse, bias, linears, taps, rate, norm_gain):
    query_lin, key_lin, value_lin, gate_lin, decay_lin, rate_lin = linears
    differentiated = inverse is not None
    queries = unit_rows(conv_head(query_lin, taps[0], masks["shifts"]))
    queries = queries * queries.shape[1] ** (-0.5)
    keys = unit_rows(conv_head(key_lin, taps[1], masks["shifts"]))
    values = conv_head(value_lin, taps[2], masks["shifts"])
    write_rate = lax.logistic(rate_lin)
    ramp = smooth_ramp if differentiated else plain_softplus
    log_decay = -rate * ramp(decay_lin + bias)
    ratio = jnp.exp(fp_dot(masks["upto"], log_decay * masks["later"], 1, 0))
    lower_part = write_rate * ratio * fp_dot(keys, keys, 1, 1) * masks["strict"]
    target = write_rate * values
    if differentiated:
        writes = apply_inverse(inverse, lower_part, target)
    else:
        inverse = unit_lower_inverse(lower_part, masks["row_index"], masks["column_index"])
        writes = fp_dot(inverse, target, 1, 0)
    heads = fp_dot(ratio * fp_dot(queries, keys, 1, 1) * masks["within"], writes, 1, 0)
    mean_square = jnp.sum(heads * heads, axis=1, keepdims=True) * (1.0 / heads.shape[1])
    normed = heads * lax.rsqrt(mean_square + epsilon) * norm_gain
    gated = normed * (gate_lin * lax.logistic(gate_lin)) * masks["inside"]
    return (gated, inverse)


def head_operands(h, heads, lin_ref, conv_refs, log_ref, bias_ref, gain_ref):
    length = lin_ref.shape[0]
    key_size = conv_refs[0].shape[1] // heads
    value_size = conv_refs[2].shape[1] // heads
    widths = (key_size, key_size, value_size, value_size)
    spans = []
    base = 0
    for width in widths:
        spans.append(slice(base + h * width, base + (h + 1) * width))
        base += heads * width
    tail = lin_ref[:, base : base + 2 * heads]
    lane = lax.broadcasted_iota(jnp.int32, tail.shape, 1)
    columns = [
        jnp.sum(jnp.where(lane == place, tail, 0.0), axis=1, keepdims=True)
        for place in (h, heads + h)
    ]
    linears = tuple(lin_ref[:, span] for span in spans) + tuple(columns)
    tap_spans = [slice(h * width, (h + 1) * width) for width in widths[:3]]
    taps = tuple(
        tuple(ref[i : i + 1, span] for i in range(ref.shape[0]))
        for ref, span in zip(conv_refs, tap_spans)
    )
    rate = jnp.exp(jnp.full((length, 1), log_ref[h], jnp.float32))
    bias = jnp.full((length, 1), bias_ref[h], jnp.float32)
    return linears, taps, rate, bias, gain_ref[...], spans, tap_spans, base


def spread_columns(columns):
    shape = (columns[0].shape[0], len(columns))
    lane = lax.broadcasted_iota(jnp.int32, shape, 1)
    total = jnp.zeros(shape, jnp.float32)
    for place, column in enumerate(columns):
        total = total + jnp.where(lane == place, column, 0.0)
    return total


def mixer_forward_kernel(
    bounds_ref, log_ref, bias_ref, lin_ref, qc_ref, kc_ref, vc_ref, gain_ref, out_ref, inverse_ref
):
    heads = log_ref.shape[0]
    conv_refs = (qc_ref, kc_ref, vc_ref)
    masks = slot_masks(bounds_ref, lin_ref.shape[0], qc_ref.shape[0])
    for h in range(heads):
        linears, taps, rate, bias, gain, _, tap_spans, _ = head_operands(
            h, heads, lin_ref, conv_refs, log_ref, bias_ref, gain_ref
        )
        gated, inverse = mixer_head(masks, None, bias, linears, taps, rate, gain)
        out_ref[:, tap_spans[2]] = gated.astype(out_ref.dtype)
        inverse_ref[h] = inverse


def mixer_backward_kernel(
    bounds_ref,
    log_ref,
    bias_ref,
    lin_ref,
    qc_ref,
    kc_ref,
    vc_ref,
    gain_ref,
    inverse_ref,
    upstream_ref,
    wire_ref,
    dq_ref,
    dk_ref,
    dv_ref,
    gain_grad_ref,
    column_ref,
):
    heads = log_ref.shape[0]
    conv_refs = (qc_ref, kc_ref, vc_ref)
    masks = slot_masks(bounds_ref, lin_ref.shape[0], qc_ref.shape[0])
    decay_columns, rate_columns, log_columns = [], [], []
    gain_total = jnp.zeros(gain_ref.shape, jnp.float32)
    for h in range(heads):
        linears, taps, rate, bias, gain, spans, tap_spans, base = head_operands(
            h, heads, lin_ref, conv_refs, log_ref, bias_ref, gain_ref
        )
        inverse = inverse_ref[h]

        def piece(linear_set, tap_set, rate_set, gain_set):
            return mixer_head(masks, inverse, bias, linear_set, tap_set, rate_set, gain_set)[0]

        _, back = jax.vjp(piece, linears, taps, rate, gain)
        grad_linears, grad_taps, grad_rate, grad_gain = back(upstream_ref[:, tap_spans[2]])
        for span, grad in zip(spans, grad_linears):
            wire_ref[:, span] = grad.astype(wire_ref.dtype)
        for ref, span, grads in zip((dq_ref, dk_ref, dv_ref), tap_spans, grad_taps):
            for i, grad in enumerate(grads):
                ref[i : i + 1, span] = grad
        gain_total = gain_total + grad_gain
        decay_columns.append(grad_linears[4])
        rate_columns.append(grad_linears[5])
        log_columns.append(grad_rate * rate)
    wire_ref[:, base : base + 2 * heads] = spread_columns(decay_columns + rate_columns).astype(
        wire_ref.dtype
    )
    column_ref[...] = spread_columns(log_columns + decay_columns)
    gain_grad_ref[...] = gain_total


def mixer_specs(count):
    return [pl.BlockSpec(memory_space=pltpu.SMEM)] * 3 + [
        pl.BlockSpec(memory_space=pltpu.VMEM)
    ] * count


def mixer_forward(bounds, projected, params):
    conv_query, conv_key, conv_value, log_rate, rate_bias, norm_gain = params
    length = projected.shape[0]
    heads = log_rate.shape[0]
    return pl.pallas_call(
        mixer_forward_kernel,
        out_shape=(
            jax.ShapeDtypeStruct((length, conv_value.shape[1]), jnp.bfloat16),
            jax.ShapeDtypeStruct((heads, length, length), jnp.float32),
        ),
        in_specs=mixer_specs(5),
        out_specs=tuple(mixer_specs(2)[3:]),
        name="mixer_forward",
    )(bounds, log_rate, rate_bias, projected, conv_query, conv_key, conv_value, norm_gain[None, :])


def mixer_backward(bounds, projected, params, inverse, upstream):
    conv_query, conv_key, conv_value, log_rate, rate_bias, norm_gain = params
    length = projected.shape[0]
    heads = log_rate.shape[0]
    wire, dq, dk, dv, dgain, columns = pl.pallas_call(
        mixer_backward_kernel,
        out_shape=(
            jax.ShapeDtypeStruct(projected.shape, jnp.bfloat16),
            jax.ShapeDtypeStruct(conv_query.shape, jnp.float32),
            jax.ShapeDtypeStruct(conv_key.shape, jnp.float32),
            jax.ShapeDtypeStruct(conv_value.shape, jnp.float32),
            jax.ShapeDtypeStruct((1, norm_gain.shape[0]), jnp.float32),
            jax.ShapeDtypeStruct((length, 2 * heads), jnp.float32),
        ),
        in_specs=mixer_specs(7),
        out_specs=tuple(mixer_specs(6)[3:]),
        name="mixer_backward",
    )(
        bounds,
        log_rate,
        rate_bias,
        projected,
        conv_query,
        conv_key,
        conv_value,
        norm_gain[None, :],
        inverse,
        upstream,
    )
    sums = jnp.sum(columns, axis=0)
    return wire, (dq, dk, dv, sums[:heads], sums[heads:], dgain[0])


def small_sum(values, axes):
    return jnp.sum(lax.all_gather(values, axes), axis=0)


def feature_total(values):
    return small_sum(values, "row")


def norm_scale(values):
    feature_count = values.shape[1] * lax.axis_size("row")
    return lax.rsqrt(feature_total(jnp.sum(values * values, axis=1)) / feature_count + epsilon)


def norm_backward(values, row_scale, gain_vector, upstream):
    feature_count = values.shape[1] * lax.axis_size("row")
    weighted = upstream * gain_vector
    inner_mean = feature_total(jnp.sum(weighted * values, axis=1)) / feature_count
    grad_values = (
        row_scale[:, None] * weighted
        - values * (row_scale * row_scale * row_scale * inner_mean)[:, None]
    )
    return (grad_values, jnp.sum(upstream * values * row_scale[:, None], axis=0))


def token_gather(values):
    return lax.all_gather(values, "col", axis=0, tiled=True)


def head_gather(values):
    return lax.all_gather(values, "row", axis=0, tiled=True)


def product_terms(left, right, flipped):
    inner_dim = 1 if flipped else 0
    return lax.dot_general(
        left, right, (((1,), (inner_dim,)), ((), ())), preferred_element_type=jnp.float32
    )


def head_sums(left, right, flipped):
    terms = product_terms(left, right, flipped)
    return lax.psum_scatter(terms, "row", scatter_dimension=0, tiled=True)


def token_sums(left, right, flipped):
    terms = product_terms(left, right, flipped)
    return lax.psum_scatter(terms, "col", scatter_dimension=0, tiled=True)


def group_sum(values):
    sent = values.astype(jnp.bfloat16)
    if lax.axis_size("dp") == 2:
        other = lax.ppermute(sent, "dp", [(0, 1), (1, 0)])
        return sent.astype(jnp.float32) + other.astype(jnp.float32)
    return lax.psum(sent, "dp").astype(jnp.float32)


def packed_psum(arrays, axes):
    flat = jnp.concatenate([array.reshape(-1) for array in arrays])
    total = small_sum(flat, axes)
    pieces = []
    start = 0
    for array in arrays:
        pieces.append(total[start : start + array.size].reshape(array.shape))
        start += array.size
    return pieces


def weight_grad(left, right):
    return lax.dot_general(
        left, right, (((0,), (0,)), ((), ())), preferred_element_type=jnp.float32
    )


def split_points(matrices):
    edges = []
    running_total = 0
    for matrix in matrices[:-1]:
        running_total = running_total + matrix.shape[1]
        edges.append(running_total)
    return edges


def shards(
    block_input,
    attn_gain,
    query_weight,
    key_weight,
    value_weight,
    gate_weight,
    decay_weight,
    beta_weight,
    query_conv,
    key_conv,
    value_conv,
    decay_log,
    decay_bias,
    head_gain,
    out_weight,
    ffn_gain,
    ffn_gate,
    ffn_up,
    ffn_down,
    out_grad,
    seq_starts,
    seq_lengths,
):
    slot_rows = block_input.shape[0]
    slot_index = lax.axis_index("dp") * lax.axis_size("col") + lax.axis_index("row")
    starts = lax.dynamic_index_in_dim(seq_starts, slot_index, 0, keepdims=False)
    lengths = lax.dynamic_index_in_dim(seq_lengths, slot_index, 0, keepdims=False)
    bounds = jnp.stack([starts, lengths])
    position = jnp.arange(slot_rows, dtype=jnp.int32)[:, None]
    inside = jnp.sum(
        ((position >= starts) & (position < starts + lengths)).astype(jnp.float32), axis=1
    )
    inputs = block_input.astype(jnp.float32)
    first_scale = norm_scale(inputs)
    first_normalized = (inputs * first_scale[:, None] * attn_gain).astype(jnp.bfloat16)
    gathered_first = token_gather(first_normalized)
    in_list = (query_weight, key_weight, value_weight, gate_weight, decay_weight, beta_weight)
    in_edges = split_points(in_list)
    in_weights = jnp.concatenate(in_list, axis=1)
    projected = head_sums(gathered_first, in_weights, False)
    mixer_params = (query_conv, key_conv, value_conv, decay_log, decay_bias, head_gain)
    mixer_output, inverse = mixer_forward(bounds, projected, mixer_params)
    mixed_rows = head_gather(mixer_output)
    resid = inputs + token_sums(mixed_rows, out_weight, False)
    second_scale = norm_scale(resid)
    second_normalized = (resid * second_scale[:, None] * ffn_gain).astype(jnp.bfloat16)
    gathered_second = token_gather(second_normalized)
    ffn_weights = jnp.concatenate([ffn_gate, ffn_up], axis=1)
    hidden_width = ffn_gate.shape[1]
    ffn_inner = head_sums(gathered_second, ffn_weights, False)
    gate_part = ffn_inner[:, :hidden_width]
    up_part = ffn_inner[:, hidden_width:]
    hidden_activation = (jax.nn.silu(gate_part) * up_part * inside[:, None]).astype(jnp.bfloat16)
    hidden_rows = head_gather(hidden_activation)
    output = (resid + token_sums(hidden_rows, ffn_down, False)).astype(jnp.bfloat16)
    grad_rows = token_gather(out_grad)
    down_grad = weight_grad(hidden_rows, grad_rows)
    grad_hidden = head_sums(grad_rows, ffn_down, True) * inside[:, None]
    sigmoid_gate = jax.nn.sigmoid(gate_part)
    gate_gradient = grad_hidden * up_part * sigmoid_gate * (1.0 + gate_part * (1.0 - sigmoid_gate))
    up_gradient = grad_hidden * gate_part * sigmoid_gate
    grad_ffn = jnp.concatenate([gate_gradient, up_gradient], axis=1).astype(jnp.bfloat16)
    grad_ffn_rows = head_gather(grad_ffn)
    ffn_weight_grad = weight_grad(gathered_second, grad_ffn_rows)
    gate_grad = ffn_weight_grad[:, :hidden_width]
    up_grad = ffn_weight_grad[:, hidden_width:]
    grad_second = token_sums(grad_ffn_rows, ffn_weights, True)
    resid_part, feedforward_gain_share = norm_backward(resid, second_scale, ffn_gain, grad_second)
    grad_resid = out_grad.astype(jnp.float32) + resid_part
    residual_signal_path = grad_resid.astype(jnp.bfloat16)
    resid_rows = token_gather(residual_signal_path)
    out_weight_grad = weight_grad(mixed_rows, resid_rows)
    grad_mixed = head_sums(resid_rows, out_weight, True)
    linear_signal_path, parameter_gradients = mixer_backward(
        bounds, projected, mixer_params, inverse, grad_mixed
    )
    lin_rows = head_gather(linear_signal_path)
    in_weight_grad = weight_grad(gathered_first, lin_rows)
    in_grads = jnp.split(in_weight_grad, in_edges, axis=1)
    grad_first = token_sums(lin_rows, in_weights, True)
    input_part, attention_gain_share = norm_backward(inputs, first_scale, attn_gain, grad_first)
    input_grad = grad_resid + input_part
    param_sums = packed_psum(parameter_gradients, ("dp", "row"))
    gain_sums = packed_psum((attention_gain_share, feedforward_gain_share), ("dp", "col"))
    head_gain_grad = small_sum(param_sums[5], "col")
    return (
        output,
        input_grad,
        gain_sums[0],
        *[group_sum(grad) for grad in in_grads],
        *param_sums[:5],
        head_gain_grad,
        group_sum(out_weight_grad),
        gain_sums[1],
        group_sum(gate_grad),
        group_sum(up_grad),
        group_sum(down_grad),
    )


def solution(mesh):
    in_specs = (
        P(("dp", "col"), "row"),
        P("row"),
        P("row", "col"),
        P("row", "col"),
        P("row", "col"),
        P("row", "col"),
        P("row", "col"),
        P("row", "col"),
        P(None, "col"),
        P(None, "col"),
        P(None, "col"),
        P("col"),
        P("col"),
        P(),
        P("col", "row"),
        P("row"),
        P("row", "col"),
        P("row", "col"),
        P("col", "row"),
        P(("dp", "col"), "row"),
        P(),
        P(),
    )
    out_specs = (
        P(("dp", "col"), "row"),
        P(("dp", "col"), "row"),
        P("row"),
        P("row", "col"),
        P("row", "col"),
        P("row", "col"),
        P("row", "col"),
        P("row", "col"),
        P("row", "col"),
        P(None, "col"),
        P(None, "col"),
        P(None, "col"),
        P("col"),
        P("col"),
        P(),
        P("col", "row"),
        P("row"),
        P("row", "col"),
        P("row", "col"),
        P("col", "row"),
    )
    return jax.shard_map(shards, mesh=mesh, in_specs=in_specs, out_specs=out_specs, check_vma=False)
```
